32 devices in a mesh: expert: 4 (over z), replica: 8 (over y, x, core).
Axes of the slice: x: 2, y: 2, z: 4, core: 2. Of those that a mesh axis runs over, the one named last changes fastest.
Arguments:
- tokens: bfloat16 [4096, 3584], P(('expert', 'replica')), may hold values from -6 to 6
- routes: int32 [4096, 2], P(('expert', 'replica')), may hold values from 0 to 3, all different within a row; in each aligned block of 128 rows (0 to 127, 128 to 255, ...) at most 128 rows name the same one
- cotangent: bfloat16 [4096, 2, 1280], P(('expert', 'replica')), may hold values from -0.08984375 to 0.08984375
- weights: bfloat16 [4, 3584, 1280], P('expert', 'replica'), may hold values from -0.09375 to 0.09375
- first_moment: float32 [4, 3584, 1280], P('expert', 'replica'), may hold values from -6 to 6
- second_moment: float32 [4, 3584, 1280], P('expert', 'replica'), may hold values from 0.25 to 4
- pairing: int32 [4], replicated, may hold values from 0 to 3, as said below
Outputs:
- activation: bfloat16 [4096, 2, 1280], P(('expert', 'replica'))
- new_weights: bfloat16 [4, 3584, 1280], P('expert', 'replica')
- new_first: float32 [4, 3584, 1280], P('expert', 'replica')
- new_second: float32 [4, 3584, 1280], P('expert', 'replica')
- update: float32 [4, 3584, 1280], P('expert', 'replica')
The draws below stay inside these ranges and needn't reach their ends.
Inputs may be any that keep to these rules, and one draw needn't show every extreme that they name: `routes`: each row names 2 different experts. Within the rows of one device no expert is named by more than 128 rows, and in every draw some device names some expert in exactly 128 rows. The experts fall into pairs: pairing[pairing[s]] == s and pairing[s] != s for every s.
All inputs are finite; a program needn't handle non-finite values.
Results may differ from the reference program's by a relative error of at most 0.0045.
Values may be sent and summed in bfloat16 or wider, within the bound.
No kernel may reach another device: no remote copies, remote signals or barrier semaphores. Data moves between devices by JAX's collectives and lax.ppermute only.
A program may use at most 128 MiB of HBM per device.

```python
import math
import jax
import jax.numpy as jnp
import numpy as np
from jax import lax

D = 3584
FW = 1280
TOP = 2
TOK_DEV = 128
EXPERTS = 4
CAP = 128
TOKENS = 4096
N_EXPERT = 4
N_REPLICA = 8


def draw_pairing(key, part):
    order = jax.random.permutation(key, EXPERTS).astype(jnp.int32)
    evens = order[0::2]
    odds = order[1::2]
    return jnp.zeros((EXPERTS,), jnp.int32).at[evens].set(odds).at[odds].set(evens)


def levels(stream_key, shape, pieces, least, largest):
    level, own = 1.0, jax.random.fold_in(stream_key, 6)
    for position, shards_of in pieces:
        steps = jnp.exp(jax.random.uniform(jax.random.fold_in(own, position), (shards_of,), jnp.float32, least / len(pieces), largest / len(pieces)))
        level = level * jnp.repeat(steps, shape[position] // shards_of).reshape([-1 if axis == position else 1 for axis in range(len(shape))])
    return level


def deal_out(own_key, own, number, rows, count, top, most, slope):
    order = jax.random.permutation(own_key, count)
    packed, usual = portions_of(count, rows * top, most, slope, True), portions_of(count, rows * top, most, slope, False)
    places = jnp.arange(count)

    def named(sizes, rotation):
        used = int((sizes > 0).sum())
        fixed = max(1, used // 4)
        shifted = fixed + (places - fixed + rotation * (used - fixed)) % max(1, count - fixed)
        return jnp.zeros((count,), jnp.int32).at[order[jnp.where(places < fixed, places, shifted)]].set(jnp.asarray(sizes, jnp.int32))

    sizes = jnp.where(number % 4 == 0, named(packed, number // 4), named(usual, number - number // 4 - 1))
    mixed = jax.random.permutation(jax.random.fold_in(own, 3), count)
    source_of, sink = mixed[0:count // 2 * 2:2], mixed[1:count // 2 * 2:2]
    slack = jnp.minimum(sizes[source_of] - 1, most - sizes[sink]) // 2
    slack = jnp.where((source_of == order[0]) | (sink == order[0]) | (sizes[sink] == 0), 0, jnp.maximum(slack, 0))
    shifted = jax.random.randint(jax.random.fold_in(own, 4), (count // 2,), 0, 1 << 20) % (slack + 1)
    sizes = sizes.at[source_of].add(-shifted).at[sink].add(shifted)
    labels = jnp.searchsorted(jnp.cumsum(sizes), jnp.arange(rows * top), side="right").astype(jnp.int32)
    grid = labels.reshape(top, rows).T
    grid = grid[jax.random.permutation(jax.random.fold_in(own, 1), rows)]
    rotation = jax.random.randint(jax.random.fold_in(own, 2), (rows, 1), 0, top)
    return jnp.take_along_axis(grid, (jnp.arange(top)[None, :] + rotation) % top, axis=1)


def portions_of(number_of, total, limit, slope, full):
    portions = [(1 << 20) // math.isqrt(standing ** slope) + 1 for standing in range(1, number_of + 1)]
    largest = limit if full else min(limit, max(-(-total // number_of), total * portions[0] // sum(portions)))
    least = 1 if total - largest >= number_of - 1 else 0
    given, rest = [largest] + [least] * (number_of - 1), total - largest - least * (number_of - 1)
    while rest > 0:
        free = [i for i in range(1, number_of) if given[i] < largest] or [i for i in range(1, number_of) if given[i] < limit]
        whole, left = sum([portions[i] for i in free]), rest
        for i in free:
            addition = min(limit - given[i], max(1, left * portions[i] // whole), rest)
            given[i] = given[i] + addition
            rest = rest - addition
    return np.array(given)


def normal_values(rng, dims, deviation, limit, split=(), kind=jnp.bfloat16):
    drawn = deviation * jax.random.normal(rng, dims, jnp.float32)
    if split:
        drawn = drawn * levels(rng, dims, split, -0.22, 0.18)
    return jnp.clip(drawn, -limit, limit).astype(kind)


def setup_inputs(seed: int = 0) -> dict:
    seeds = jax.random.split(jax.random.key(seed), 8)
    tokens = normal_values(seeds[0], (TOKENS, D), 1.0, 6.0, ((0, 32),))
    routes_keys = jax.random.split(jax.random.fold_in(seeds[1], 1), TOKENS // TOK_DEV)
    routes_turns = jax.random.permutation(jax.random.fold_in(seeds[1], 3), TOKENS // TOK_DEV)
    routes = jax.vmap(lambda own, number: deal_out(jax.random.fold_in(seeds[1], 2), own, number, TOK_DEV, EXPERTS, TOP, CAP, 2))(routes_keys, routes_turns).reshape((TOKENS, TOP))
    cotangent = normal_values(seeds[2], (TOKENS, TOP, FW), 0.015625, 0.08984375, ((0, 32),))
    weights = normal_values(seeds[3], (EXPERTS, D, FW), D ** -0.5, 0.09375, ((0, 4), (1, 8)))
    first_moment = normal_values(seeds[4], (EXPERTS, D, FW), 1.0, 6.0, ((0, 4), (1, 8)), jnp.float32)
    second_moment = jnp.clip(jnp.exp(math.log(4.0) - 2.7725887 * jax.random.uniform(seeds[5], (EXPERTS, D, FW), jnp.float32) ** levels(seeds[5], (EXPERTS, D, FW), ((0, 4), (1, 8)), -0.2, 0.2)), 0.25, 4.0)
    pairing = draw_pairing(jax.random.fold_in(seeds[7], 71), 0)
    return dict(tokens=tokens, routes=routes, cotangent=cotangent, weights=weights, first_moment=first_moment, second_moment=second_moment, pairing=pairing)


BETA_ONE = 0.8
BETA_TWO = 0.9
EPSILON = 1e-08

def reference(tokens, routes, cotangent, weights, first_moment, second_moment, pairing):
    group_tokens = N_EXPERT * TOK_DEV
    route_count = group_tokens * TOP
    bucket = N_EXPERT * CAP
    token_blocks = tokens.reshape(N_EXPERT, N_REPLICA, TOK_DEV, D).transpose(1, 0, 2, 3)
    route_blocks = routes.reshape(N_EXPERT, N_REPLICA, TOK_DEV, TOP).transpose(1, 0, 2, 3)
    grad_blocks = cotangent.reshape(N_EXPERT, N_REPLICA, TOK_DEV, TOP, FW).transpose(1, 0, 2, 3, 4)
    expert_ids = jnp.arange(EXPERTS, dtype=jnp.int32)

    def one_expert(operands):
        expert_rows, expert_grads, expert_weight = operands
        projected = jnp.dot(expert_rows, expert_weight, preferred_element_type=jnp.float32)
        partial_value = jnp.dot(expert_rows.T, expert_grads, preferred_element_type=jnp.float32)
        return (projected.astype(jnp.bfloat16), partial_value.astype(jnp.bfloat16))

    def one_group(running, group):
        group_rows, group_routes, group_grads = group
        group_rows = group_rows.reshape(group_tokens, D)
        flat_routes = group_routes.reshape(route_count).astype(jnp.int32)
        flat_grads = group_grads.reshape(route_count, FW)
        one_hot = (flat_routes[:, None] == expert_ids[None, :]).astype(jnp.int32)
        places = lax.optimization_barrier(jnp.sum((jnp.cumsum(one_hot, axis=0) - 1) * one_hot, axis=1)).astype(jnp.int32)
        table = jnp.full((EXPERTS, bucket), route_count, jnp.int32)
        table = table.at[flat_routes, places].set(jnp.arange(route_count, dtype=jnp.int32))
        token_index = jnp.where(table < route_count, table // TOP, group_tokens).astype(jnp.int32)
        padded_rows = jnp.concatenate([group_rows, jnp.zeros((1, D), group_rows.dtype)], axis=0)
        padded_grads = jnp.concatenate([flat_grads, jnp.zeros((1, FW), flat_grads.dtype)], axis=0)
        projected, partial_value = lax.map(one_expert, (padded_rows[token_index], padded_grads[table], weights))
        activation = projected[flat_routes, places].reshape(N_EXPERT, TOK_DEV, TOP, FW)
        partial_value = lax.optimization_barrier(partial_value)
        return (running + partial_value.astype(jnp.float32), activation)
    start = jnp.zeros((EXPERTS, D, FW), jnp.float32)
    gradient, activation = lax.scan(one_group, start, (token_blocks, route_blocks, grad_blocks))
    activation = activation.transpose(1, 0, 2, 3, 4).reshape(TOKENS, TOP, FW)
    new_weights = weights[pairing]
    moved_grad = gradient[pairing]
    new_first = BETA_ONE * first_moment[pairing] + (1.0 - BETA_ONE) * moved_grad
    new_second = BETA_TWO * second_moment[pairing] + (1.0 - BETA_TWO) * moved_grad * moved_grad
    update = new_first / (jnp.sqrt(new_second) + EPSILON)
    return (activation, new_weights, new_first, new_second, update)
```

```python
import math

import jax
import jax.numpy as jnp
from jax import lax
from jax.experimental import pallas as pl
from jax.experimental.pallas import tpu as pltpu
from jax.sharding import PartitionSpec as P

BETA_ONE = 0.8
BETA_TWO = 0.9
EPSILON = 1e-08


STATE_TYPE = jnp.bfloat16


def relocate(block, pairing):
    slot_count = pairing.shape[0]
    pieces = block.reshape(slot_count, block.shape[1] // slot_count, block.shape[2])
    spread = lax.all_to_all(pieces, "expert", split_axis=0, concat_axis=0, tiled=True)
    chosen = jnp.take(spread, pairing, axis=0)
    settled = lax.all_to_all(chosen, "expert", split_axis=0, concat_axis=0, tiled=True)
    return settled.reshape(block.shape)


def adam(first, second, gradient):
    new_first = BETA_ONE * first + (1.0 - BETA_ONE) * gradient
    new_second = BETA_TWO * second + (1.0 - BETA_TWO) * gradient * gradient
    return new_first, new_second, new_first / (jnp.sqrt(new_second) + EPSILON)


def general_body(tokens, routes, cotangent, weights, first_moment, second_moment, pairing):
    slot_count = pairing.shape[0]
    tok_rows, choose_count = routes.shape
    hidden_width = cotangent.shape[2]
    model_width = tokens.shape[1]
    capacity = 2 * tok_rows * choose_count // slot_count
    flat_routes = routes.reshape(-1)
    one_hot = (flat_routes[:, None] == jnp.arange(slot_count, dtype=jnp.int32)[None, :]).astype(
        jnp.int32
    )
    places = jnp.sum((jnp.cumsum(one_hot, axis=0) - 1) * one_hot, axis=1)
    weights = relocate(weights, pairing)
    first_moment = relocate(first_moment, pairing)
    second_moment = relocate(second_moment, pairing)
    owners = jnp.take(pairing, flat_routes)
    targets = owners * capacity + places
    sources = jnp.arange(tok_rows * choose_count, dtype=jnp.int32) // choose_count

    def dispatch(rows):
        width = rows.shape[1]
        sent = jnp.zeros((slot_count * capacity, width), jnp.bfloat16).at[targets].set(rows)
        came = lax.all_to_all(
            sent.reshape(slot_count, capacity, width), "expert", split_axis=0, concat_axis=0, tiled=True
        )
        return came.reshape(slot_count * capacity, width)

    came_rows = dispatch(tokens[sources])
    came_grads = dispatch(cotangent.reshape(-1, hidden_width))
    weight_shard = weights.reshape(weights.shape[1], hidden_width)
    projected = jnp.dot(
        came_rows,
        lax.all_gather(weight_shard, "replica", axis=0, tiled=True),
        preferred_element_type=jnp.float32,
    ).astype(jnp.bfloat16)
    returned = lax.all_to_all(
        projected.reshape(slot_count, capacity, hidden_width),
        "expert",
        split_axis=0,
        concat_axis=0,
        tiled=True,
    )
    activation = returned.reshape(slot_count * capacity, hidden_width)[targets].reshape(
        tok_rows, choose_count, hidden_width
    )
    gradient = lax.psum_scatter(
        lax.dot_general(
            came_rows, came_grads, (((0,), (0,)), ((), ())), preferred_element_type=jnp.float32
        ).astype(jnp.bfloat16),
        "replica",
        scatter_dimension=0,
        tiled=True,
    ).astype(jnp.float32)
    return (activation, weights) + adam(first_moment, second_moment, gradient.reshape(first_moment.shape))


def project_kernel(rows, model, width):
    half = rows // 2

    def kernel(x_own, x_mate, *refs):
        pieces, out, full, xs, sems = refs[:16], refs[16], refs[17], refs[18], refs[19]
        place = lax.axis_index("replica")
        chip, core = place // 2, place % 2
        copies = []
        for j in range(4):
            base = jnp.bitwise_xor(chip, j) * (2 * rows)
            for side in range(2):
                for part in range(2):
                    at = base + (core if side == 0 else 1 - core) * rows + part * half
                    at = pl.multiple_of(at, half)
                    n = (j * 2 + side) * 2 + part
                    copy = pltpu.make_async_copy(pieces[n], full.at[pl.ds(at, half), :], sems.at[n])
                    copy.start()
                    copies.append(copy)
        tok = x_own.shape[0]
        xs[:tok, :] = x_own[...]
        xs[tok:, :] = x_mate[...]
        for copy in copies:
            copy.wait()
        out[...] = jnp.dot(xs[...], full[...], preferred_element_type=jnp.float32).astype(out.dtype)

    def call(x_own, x_mate, pieces):
        tok = x_own.shape[0]
        vmem = pl.BlockSpec(memory_space=pltpu.VMEM)
        return pl.pallas_call(
            kernel,
            out_shape=jax.ShapeDtypeStruct((2 * tok, width), jnp.bfloat16),
            in_specs=[vmem, vmem] + [pl.BlockSpec(memory_space=pl.ANY)] * 16,
            out_specs=vmem,
            scratch_shapes=[
                pltpu.VMEM((model, width), jnp.bfloat16),
                pltpu.VMEM((2 * tok, model), jnp.bfloat16),
                pltpu.SemaphoreType.DMA((16,)),
            ],
            cost_estimate=pl.CostEstimate(
                flops=4 * tok * model * width, transcendentals=0, bytes_accessed=2 * model * width
            ),
            name="project",
        )(x_own, x_mate, *pieces)

    return call


def gradient_call(x, cot, place, rows):
    tok, model = x.shape
    width = cot.shape[1]
    half = rows // 2

    def kernel(place_ref, x_ref, cot_ref, keep_a, keep_b, send_a, send_b):
        block = lax.dot_general(
            x_ref[...], cot_ref[...], (((0,), (0,)), ((), ())), preferred_element_type=jnp.float32
        ).astype(jnp.bfloat16)
        core = place_ref[0] % 2

        def put(first, second):
            first[0][0] = block[:half]
            first[1][0] = block[half:rows]
            second[0][0] = block[rows : rows + half]
            second[1][0] = block[rows + half :]

        @pl.when(core == 0)
        def _():
            put((keep_a, keep_b), (send_a, send_b))

        @pl.when(core == 1)
        def _():
            put((send_a, send_b), (keep_a, keep_b))

    piece = jax.ShapeDtypeStruct((4, half, width), jnp.bfloat16)
    a_spec = pl.BlockSpec((1, half, width), lambda j, p: ((j // 2) + 2 * (j % 2), 0, 0))
    b_spec = pl.BlockSpec((1, half, width), lambda j, p: (j, 0, 0))
    return pl.pallas_call(
        kernel,
        out_shape=(piece, piece, piece, piece),
        grid_spec=pltpu.PrefetchScalarGridSpec(
            num_scalar_prefetch=1,
            grid=(4,),
            in_specs=[
                pl.BlockSpec((tok, 2 * rows), lambda j, p: (0, jnp.bitwise_xor(p[0] // 2, j))),
                pl.BlockSpec((tok, width), lambda j, p: (0, 0)),
            ],
            out_specs=[a_spec, b_spec, a_spec, b_spec],
        ),
        cost_estimate=pl.CostEstimate(
            flops=2 * tok * model * width, transcendentals=0, bytes_accessed=2 * model * width
        ),
        name="gradient",
    )(place, x, cot)


def add(*parts):
    total = parts[0].astype(jnp.float32)
    for part in parts[1:]:
        total = total + part.astype(jnp.float32)
    return total


def after(value, *others):
    return lax.optimization_barrier((value,) + others)[0]


def paired_body(pair, mate, tokens, routes, cotangent, weights, first_moment, second_moment):
    slots = lax.axis_size("expert")
    replicas = lax.axis_size("replica")
    slot = lax.axis_index("expert")
    place = lax.axis_index("replica")
    rows, width = weights.shape[1:]
    model = tokens.shape[1]
    half = rows // 2

    def hop(value, step):
        return lax.ppermute(value, "expert", [(i, i ^ step) for i in range(slots)])

    def rep(value, step):
        return lax.ppermute(value, "replica", [(i, i ^ step) for i in range(replicas)])

    def gather(a, b):
        xa, xb, ya, yb = rep(a, 2), rep(b, 2), rep(a, 4), rep(b, 4)
        da, db = rep(ya, 2), rep(xb, 4)
        pieces = []
        for one, two in ((a, b), (xa, xb), (ya, yb), (da, db)):
            pieces += [one, two, rep(one, 1), rep(two, 1)]
        return pieces

    def spread(keep_a, keep_b, send_a, send_b):
        came_a, came_b = rep(send_a, 1), rep(send_b, 1)
        out_xa = add(keep_a[2:], came_a[2:]).astype(jnp.bfloat16)
        out_yb = add(keep_b[2:], came_b[2:]).astype(jnp.bfloat16)
        in_xa, in_yb = rep(out_xa, 2), rep(out_yb, 4)
        out_ya = add(keep_a[1], came_a[1], in_xa[1]).astype(jnp.bfloat16)
        out_xb = add(keep_b[1], came_b[1], in_yb[1]).astype(jnp.bfloat16)
        in_ya, in_xb = rep(out_ya, 4), rep(out_xb, 2)
        return (
            (keep_a[0], came_a[0], in_xa[0], in_ya),
            (keep_b[0], came_b[0], in_yb[0], in_xb),
        )

    weight = weights[0]
    mate_tokens = hop(tokens, mate)
    mate_routes = hop(routes, mate)
    mate_cotangent = hop(cotangent, mate)
    new_weight = hop(weight, pair)
    home_pieces = gather(weight[:half], weight[half:])

    home, other = slot, jnp.bitwise_xor(slot, pair)
    x = jnp.concatenate([tokens, mate_tokens], axis=0)
    all_cot = jnp.concatenate([cotangent, mate_cotangent], axis=0)
    all_routes = jnp.concatenate([routes, mate_routes], axis=0)

    def cot_of(expert):
        picked = jnp.where((all_routes == expert)[:, :, None], all_cot, jnp.zeros_like(all_cot))
        return jnp.sum(picked.astype(jnp.float32), axis=1).astype(jnp.bfloat16)

    where = place.astype(jnp.int32).reshape(1)
    home_parts = gradient_call(x, cot_of(home), where, rows)
    other_parts = gradient_call(x, cot_of(other), where, rows)

    state = after(first_moment[0], new_weight).astype(STATE_TYPE)
    moved_first = hop(state, pair)
    moved_second = hop(second_moment[0].astype(STATE_TYPE), pair)

    home_a, home_b = spread(*home_parts)
    theirs_a = hop(add(*home_a).astype(jnp.bfloat16), pair)
    theirs_b = hop(add(*home_b).astype(jnp.bfloat16), pair)

    project = project_kernel(rows, model, width)
    home_out = project(tokens, mate_tokens, home_pieces)
    new_pieces = gather(new_weight[:half], new_weight[half:])
    other_out = project(tokens, mate_tokens, new_pieces)

    tok = tokens.shape[0]

    def pick(which, home_rows, other_rows, rest):
        return jnp.where(
            (which == home)[:, :, None],
            home_rows[:, None, :],
            jnp.where((which == other)[:, :, None], other_rows[:, None, :], rest),
        )

    back = pick(mate_routes, home_out[tok:], other_out[tok:], jnp.zeros_like(cotangent))
    activation = pick(routes, home_out[:tok], other_out[:tok], hop(back, mate))

    other_a, other_b = spread(*other_parts)
    gradient = jnp.concatenate([add(*other_a, theirs_a), add(*other_b, theirs_b)], axis=0)
    moments = adam(moved_first.astype(jnp.float32), moved_second.astype(jnp.float32), gradient)
    return (activation, new_weight[None]) + tuple(value[None] for value in moments)


def paired_program(tokens, routes, cotangent, weights, first_moment, second_moment, pairing):
    slots = pairing.shape[0]
    branches = []
    for pair in range(1, slots):
        mate = 2 if pair == 1 else 1
        branches.append(
            lambda *args, pair=pair, mate=mate: paired_body(pair, mate, *args)
        )
    return lax.switch(
        pairing[0] - 1, branches, tokens, routes, cotangent, weights, first_moment, second_moment
    )


def solution(mesh):
    in_specs = (
        P(("expert", "replica"), None),
        P(("expert", "replica"), None),
        P(("expert", "replica"), None, None),
        P("expert", "replica", None),
        P("expert", "replica", None),
        P("expert", "replica", None),
        P(),
    )
    out_specs = (
        P(("expert", "replica"), None, None),
        P("expert", "replica", None),
        P("expert", "replica", None),
        P("expert", "replica", None),
        P("expert", "replica", None),
    )
    slots, replicas = mesh.shape["expert"], mesh.shape["replica"]
    cube = slots == 4 and replicas == 8
    body = paired_program if cube else general_body
    return jax.shard_map(body, mesh=mesh, in_specs=in_specs, out_specs=out_specs, check_vma=False)
```
